32 devices in a mesh: dp: 4 (over y, x), seq: 8 (over z, core).
Axes of the slice: x: 2, y: 2, z: 4, core: 2. Of those that a mesh axis runs over, the one named last changes fastest.
Arguments:
- query_rows: bfloat16 [4, 1024, 1536], P('dp', 'seq'), may hold values from -6 to 6
- key_rows: bfloat16 [4, 1024, 1536], P('dp', 'seq'), may hold values from -6 to 6
- value_rows: bfloat16 [4, 1024, 1536], P('dp', 'seq'), may hold values from -6 to 6
- out_grad: bfloat16 [4, 1024, 1536], P('dp', 'seq'), may hold values from -36 to 36
- query_gain: float32 [128], replicated, may hold values from 0.5 to 5.5
- key_gain: float32 [128], replicated, may hold values from 0.5 to 5.5
- lengths: int32 [4, 16], P('dp'), may hold values from 1 to 128, 1024 in all within a row
Outputs:
- query_grad: bfloat16 [4, 1024, 1536], P('dp', 'seq')
- key_grad: bfloat16 [4, 1024, 1536], P('dp', 'seq')
- value_grad: bfloat16 [4, 1024, 1536], P('dp', 'seq')
- gain_grads: float32 [2, 128], replicated
The draws below stay inside these ranges and needn't reach their ends.
Inputs may be any that keep to these rules, and one draw needn't show every extreme that they name: The 16 lengths of a pack sum to 1024, and some sample of every pack has exactly 128 tokens.
All inputs are finite; a program needn't handle non-finite values.
Results may differ from the reference program's by a relative error of at most 0.023.
The reference program's roundings to bfloat16 on the way count: a program that leaves them out, or rounds other values in their place, can miss the bound.
Values may be sent and summed in bfloat16 or wider, within the bound.
A program may use at most 64 MiB of HBM per device.

```python
import math
import jax
import jax.numpy as jnp
import numpy as np
from jax import lax

H = 12
DH = 128
SPAN = 1
TOK_DEV = 128
REACH = 128
PACKS = 4
PACK = 1024
NSAMP = 16
N_SEQ = 8


def key_field(key):
    field = jax.random.normal(jax.random.fold_in(key, 101), (PACKS, PACK, H * DH), jnp.float32)
    return jnp.clip(field, -6.0, 6.0)


def draw_key_rows(key, part):
    return key_field(key).astype(jnp.bfloat16)


def draw_query_rows(key, part):
    sampled = jax.random.normal(jax.random.fold_in(key, 107), (PACKS, PACK, H * DH), jnp.float32)
    return jnp.clip(sampled, -6.0, 6.0).astype(jnp.bfloat16)


def draw_out_grad(key, part):
    sampled = jnp.clip(jax.random.normal(jax.random.fold_in(key, 127), (PACKS, PACK, H * DH), jnp.float32), -4.0, 4.0)
    position = (jnp.arange(PACKS)[:, None] * PACK + jnp.arange(PACK)[None, :]).astype(jnp.float32) / (PACKS * PACK)
    factor = 3.0 ** position
    return (sampled * factor[:, :, None]).astype(jnp.bfloat16)


def gain_field(key, salt):
    spread = jax.random.uniform(jax.random.fold_in(key, salt), (DH,), jnp.float32)
    return 0.5 + spread


def draw_query_gain(key, part):
    return gain_field(key, 109)


def draw_key_gain(key, part):
    return gain_field(key, 113)


def level_of(stream_key, shape, pieces, low, largest):
    def one(axis_at, blocks):
        draws = jax.random.uniform(jax.random.fold_in(jax.random.fold_in(stream_key, 6), axis_at), (blocks,), jnp.float32, low / len(pieces), largest / len(pieces))
        return jnp.repeat(jnp.exp(draws), shape[axis_at] // blocks).reshape((-1,) + (1,) * (len(shape) - axis_at - 1))

    factor_of = one(*pieces[0])
    for cut in pieces[1:]:
        factor_of = factor_of * one(*cut)
    return factor_of


def length_profile(number_of, total, bound, skew):
    loads = [(1 << 20) // math.isqrt(rank ** skew) + 1 for rank in range(2, number_of + 1)]
    rest, holding = total - bound - (number_of - 1), [1] * (number_of - 1)
    while rest > 0:
        free = [i for i in range(number_of - 1) if holding[i] < bound]
        pool, left = sum([loads[i] for i in free]), rest
        for i in free:
            more = min(bound - holding[i], max(1, left * loads[i] // pool), rest)
            holding[i] = holding[i] + more
            rest = rest - more
    return np.array([bound] + holding)


def uneven_parts(key, count, total, bound, slope):
    if count == 2:
        one = jax.random.randint(key, (), max(1, total - bound), min(bound, total - 1) + 1)
        return jnp.stack([one, total - one])
    sizes = jnp.asarray(length_profile(count, total, bound, slope), jnp.int32)
    couples = (count - 1) // 2
    giver, receiver = sizes[1:1 + 2 * couples:2], sizes[2:2 + 2 * couples:2]
    room = jnp.minimum(giver - 1, bound - receiver)
    passed = jax.random.randint(jax.random.fold_in(key, 1), (couples,), 0, 1 << 20) % (room + 1)
    sizes = sizes.at[1:1 + 2 * couples:2].set(giver - passed).at[2:2 + 2 * couples:2].set(receiver + passed)
    return sizes[jax.random.permutation(jax.random.fold_in(key, 2), count)]


def scatter_about(stream_key, shape, scale, most, pieces=(), kind=jnp.bfloat16):
    values = jax.random.normal(stream_key, shape, jnp.float32) * scale
    if len(pieces) > 0:
        values = level_of(stream_key, shape, pieces, -0.22, 0.18) * values
    return jnp.clip(values, min=-most, max=most).astype(kind)


def setup_inputs(seed: int = 0) -> dict:
    arg_keys = jax.random.split(jax.random.key(seed), 8)
    query_rows = draw_query_rows(jax.random.fold_in(arg_keys[7], 71), 0)
    key_rows = draw_key_rows(jax.random.fold_in(arg_keys[7], 71), 0)
    value_rows = scatter_about(arg_keys[2], (PACKS, PACK, H * DH), 1.0, 6.0, ((0, 4), (1, 8)))
    out_grad = draw_out_grad(jax.random.fold_in(arg_keys[7], 71), 0)
    query_gain = draw_query_gain(jax.random.fold_in(arg_keys[7], 71), 0)
    key_gain = draw_key_gain(jax.random.fold_in(arg_keys[7], 71), 0)
    lengths = jax.vmap(lambda own: uneven_parts(own, NSAMP, PACK, REACH, 2))(jax.random.split(arg_keys[6], PACKS)).reshape((PACKS, NSAMP)).astype(jnp.int32)
    return dict(query_rows=query_rows, key_rows=key_rows, value_rows=value_rows, out_grad=out_grad, query_gain=query_gain, key_gain=key_gain, lengths=lengths)


EPSILON = 1e-06
MASKED = -1e+30

def product(pattern, left_side, right_side):
    return jnp.einsum(pattern, left_side.astype(jnp.float32), right_side.astype(jnp.float32))

def normalize(entries, norm_gain):
    row_count = entries.shape[0]
    widened = entries.astype(jnp.float32).reshape(row_count, H, DH)
    inverse = lax.rsqrt(lax.optimization_barrier(jnp.mean(widened * widened, axis=2, keepdims=True)) + EPSILON)
    unit_rows = widened * inverse
    return ((unit_rows * norm_gain).astype(jnp.bfloat16).reshape(row_count, H * DH), unit_rows, inverse)

def norm_back(grad_rows, unit_rows, inverse, norm_gain):
    scaled = grad_rows * norm_gain
    inner_mean = lax.optimization_barrier(jnp.mean(scaled * unit_rows, axis=2, keepdims=True))
    result = inverse * (scaled - unit_rows * inner_mean)
    return (result.reshape(grad_rows.shape[0], H * DH).astype(jnp.bfloat16), lax.optimization_barrier(jnp.sum(grad_rows * unit_rows, axis=(0, 1))))

def segment_of(positions, lengths, extent):
    sample_ends = jnp.cumsum(lengths)
    number = lax.optimization_barrier(jnp.sum((sample_ends[None, :] <= positions[:, None]).astype(jnp.int32), axis=1))
    inside = (positions >= 0) & (positions < extent)
    return jnp.where(inside, number, -1)

def forward_band(queries, band_keys, band_values, seg_query, seg_band):
    row_count = queries.shape[0]
    factor = DH ** (-0.5)
    scores = product('qhd,khd->hqk', queries.reshape(row_count, H, DH), band_keys.reshape(-1, H, DH)) * factor
    matching = seg_query[:, None] == seg_band[None, :]
    scores = jnp.where(matching[None], scores, MASKED)
    highest = lax.optimization_barrier(jnp.max(scores, axis=2, keepdims=True))
    summed = lax.optimization_barrier(jnp.sum(jnp.exp(scores - highest), axis=2, keepdims=True))
    log_total = highest + jnp.log(summed)
    weights = jnp.exp(scores - log_total)
    weights_half = weights.astype(jnp.bfloat16)
    attended = product('hqk,khd->qhd', weights_half, band_values.reshape(-1, H, DH)).astype(jnp.bfloat16)
    return (weights, weights_half, log_total, attended)

def backward_band(queries, band_keys, band_values, grad_out, weights, weights_half, attended):
    row_count = queries.shape[0]
    factor = DH ** (-0.5)
    grad_heads = grad_out.reshape(row_count, H, DH)
    row_dot = lax.optimization_barrier(jnp.sum(grad_heads.astype(jnp.float32) * attended.astype(jnp.float32), axis=2))
    row_dot = jnp.transpose(row_dot)[:, :, None]
    grad_weights = product('qhd,khd->hqk', grad_heads, band_values.reshape(-1, H, DH))
    grad_scores = (weights * (grad_weights - row_dot)).astype(jnp.bfloat16)
    grad_query = product('hqk,khd->qhd', grad_scores, band_keys.reshape(-1, H, DH)) * factor
    key_terms = product('hqk,qhd->khd', grad_scores, queries.reshape(row_count, H, DH)) * factor
    value_terms = product('hqk,qhd->khd', weights_half, grad_heads)
    return (grad_query, key_terms, value_terms)

def gather_rims(terms):
    blocks = terms.shape[0]
    split = terms.reshape(blocks, 2 * SPAN + 1, TOK_DEV, H, DH)
    summed = split[:, SPAN]
    for step in range(2 * SPAN + 1):
        if step != SPAN:
            move = step - SPAN
            piece = split[:, step]
            zeros = jnp.zeros_like(piece[:abs(move)])
            if move > 0:
                moved = jnp.concatenate([zeros, piece[:-move]], axis=0)
            else:
                moved = jnp.concatenate([piece[-move:], zeros], axis=0)
            summed = summed + moved
    return summed.reshape(PACK, H, DH)

def reference(query_rows, key_rows, value_rows, out_grad, query_gain, key_gain, lengths):

    def one_pack(operands):
        queries_in, keys_in, values_in, grads_in, pack_lengths = operands
        positions = jnp.arange(PACK, dtype=jnp.int32)
        segments = segment_of(positions, pack_lengths, PACK)
        q_norm, q_unit, q_inverse = normalize(queries_in, query_gain)
        k_norm, k_unit, k_inverse = normalize(keys_in, key_gain)
        zero_rows = jnp.zeros((REACH, H * DH), jnp.bfloat16)
        keys_padded = jnp.concatenate([zero_rows, k_norm, zero_rows], axis=0)
        values_padded = jnp.concatenate([zero_rows, values_in, zero_rows], axis=0)
        edge_segments = jnp.full((REACH,), -1, jnp.int32)
        seg_padded = jnp.concatenate([edge_segments, segments, edge_segments], axis=0)

        def one_block(block_index):
            block_start = (block_index * TOK_DEV).astype(jnp.int32)
            queries = lax.dynamic_slice_in_dim(q_norm, block_start, TOK_DEV, 0)
            grads = lax.dynamic_slice_in_dim(grads_in, block_start, TOK_DEV, 0)
            seg_query = lax.dynamic_slice_in_dim(segments, block_start, TOK_DEV, 0)
            band_keys = lax.dynamic_slice_in_dim(keys_padded, block_start, TOK_DEV + 2 * REACH, 0)
            band_values = lax.dynamic_slice_in_dim(values_padded, block_start, TOK_DEV + 2 * REACH, 0)
            seg_band = lax.dynamic_slice_in_dim(seg_padded, block_start, TOK_DEV + 2 * REACH, 0)
            weights, weights_half, log_total, attended = forward_band(queries, band_keys, band_values, seg_query, seg_band)
            return backward_band(queries, band_keys, band_values, grads, weights, weights_half, attended)
        grad_query, key_terms, value_terms = lax.map(one_block, jnp.arange(N_SEQ, dtype=jnp.int32))
        d_query, q_gain_grad = norm_back(grad_query.reshape(PACK, H, DH), q_unit, q_inverse, query_gain)
        d_key, k_gain_grad = norm_back(gather_rims(key_terms), k_unit, k_inverse, key_gain)
        d_value = gather_rims(value_terms).reshape(PACK, H * DH).astype(jnp.bfloat16)
        return (d_query, d_key, d_value, jnp.stack([q_gain_grad, k_gain_grad]))
    query_grad, key_grad, value_grad, gain_parts = lax.map(one_pack, (query_rows, key_rows, value_rows, out_grad, lengths))
    return (query_grad, key_grad, value_grad, lax.optimization_barrier(jnp.sum(gain_parts, axis=0)))
```

```python
import functools

import jax
import jax.numpy as jnp
from jax import lax
from jax.experimental import pallas as pl
from jax.experimental.pallas import tpu as pltpu
from jax.sharding import PartitionSpec as P

DH = 128
EPSILON = 1e-06
MASKED = -1e30
HEADS_STEP = 2


def norm_back(grad, unit, inverse, gain):
    scaled = grad * gain
    inner = jnp.mean(scaled * unit, axis=1, keepdims=True)
    return (inverse * (scaled - unit * inner)).astype(jnp.bfloat16)


def kernel(
    rows, width, samples, n_seq, n_dp,
    q_ref, k_ref, v_ref, g_ref, qgain_ref, kgain_ref, len_ref,
    dq_ref, dk_ref, dv_ref, gain_ref,
    win, bias, owned, own_out, ret_send, ret_recv, gain_acc, seq_gain, dp_gain,
    load_sem, send_sem, recv_sem, back_send_sem, back_recv_sem, store_sem,
    seq_send_sem, seq_recv_sem, dp_send_sem, dp_recv_sem,
):
    half = rows // 2
    window = 2 * rows
    cols_step = HEADS_STEP * DH
    steps = width // cols_step
    factor = DH ** (-0.5)
    me = lax.axis_index("seq")
    my_dp = lax.axis_index("dp")
    has_left = me > 0
    has_right = me < n_seq - 1
    inputs = (q_ref, k_ref, v_ref, g_ref)
    outputs = (dq_ref, dk_ref, dv_ref)

    barrier = pltpu.get_barrier_semaphore()
    for d in range(1, n_seq):
        pl.semaphore_signal(barrier, inc=1, device_id={"seq": lax.rem(me + d, n_seq)})
    for d in range(1, n_dp):
        pl.semaphore_signal(barrier, inc=1, device_id={"dp": lax.rem(my_dp + d, n_dp)})

    loads = [
        pltpu.make_async_copy(ref.at[0], win.at[a, pl.ds(half, rows)], load_sem.at[a])
        for a, ref in enumerate(inputs)
    ]
    for load in loads:
        load.start()
    pl.semaphore_wait(barrier, n_seq + n_dp - 2)

    def columns(step):
        return pl.ds(pl.multiple_of(step * cols_step, cols_step), cols_step)

    def to_left(a, step):
        return pltpu.make_async_remote_copy(
            inputs[a].at[0, pl.ds(0, half), columns(step)],
            win.at[a, pl.ds(half + rows, half), columns(step)],
            send_sem.at[step, a, 0], recv_sem.at[step, a, 1],
            device_id={"seq": me - 1},
        )

    def to_right(a, step):
        return pltpu.make_async_remote_copy(
            inputs[a].at[0, pl.ds(half, half), columns(step)],
            win.at[a, pl.ds(0, half), columns(step)],
            send_sem.at[step, a, 1], recv_sem.at[step, a, 0],
            device_id={"seq": me + 1},
        )

    def back_left(step):
        return pltpu.make_async_remote_copy(
            ret_send.at[0, :, :, columns(step)],
            ret_recv.at[1, :, :, columns(step)],
            back_send_sem.at[step, 0], back_recv_sem.at[step, 1],
            device_id={"seq": me - 1},
        )

    def back_right(step):
        return pltpu.make_async_remote_copy(
            ret_send.at[1, :, :, columns(step)],
            ret_recv.at[0, :, :, columns(step)],
            back_send_sem.at[step, 1], back_recv_sem.at[step, 0],
            device_id={"seq": me + 1},
        )

    @pl.loop(0, steps)
    def _(step):
        @pl.when(has_right)
        def _():
            for a in range(4):
                to_right(a, step).start()

        @pl.when(has_left)
        def _():
            for a in range(4):
                to_left(a, step).start()

    @pl.when(jnp.logical_not(has_left))
    def _():
        win[:, 0:half, :] = jnp.zeros((4, half, width), jnp.bfloat16)
        ret_recv[0] = jnp.zeros((3, half, width), jnp.bfloat16)

    @pl.when(jnp.logical_not(has_right))
    def _():
        win[:, half + rows:, :] = jnp.zeros((4, half, width), jnp.bfloat16)
        ret_recv[1] = jnp.zeros((3, half, width), jnp.bfloat16)

    first = me * rows
    base = first - half
    far = rows * n_seq + window
    pos_col = base + lax.broadcasted_iota(jnp.int32, (window, 1), 0)
    pos_row = base + lax.broadcasted_iota(jnp.int32, (1, window), 1)
    start_col = jnp.where(pos_col >= 0, 0, -far)
    start_row = jnp.where(pos_row >= 0, 0, -far)
    end_col = jnp.full((window, 1), far, jnp.int32)
    total = jnp.int32(0)
    for s in range(samples):
        total = total + len_ref[0, s]
        start_col = jnp.where(total <= pos_col, total, start_col)
        start_row = jnp.where(total <= pos_row, total, start_row)
        end_col = jnp.where(total > pos_col, jnp.minimum(end_col, total), end_col)
    anchor = jnp.minimum(start_col + half, end_col - 1)
    mine = (anchor >= first) & (anchor < first + rows)
    owned[...] = jnp.where(mine, 1.0, 0.0)
    bias[...] = jnp.where(start_col == start_row, 0.0, MASKED)
    gain_acc[...] = jnp.zeros_like(gain_acc)

    for load in loads:
        load.wait()

    def one_head(head):
        cols = pl.ds(pl.multiple_of(head * DH, DH), DH)
        q_gain = qgain_ref[...]
        k_gain = kgain_ref[...]
        q = win[0, :, cols].astype(jnp.float32)
        k = win[1, :, cols].astype(jnp.float32)
        v = win[2, :, cols]
        grad = win[3, :, cols]
        q_inv = lax.rsqrt(jnp.mean(q * q, axis=1, keepdims=True) + EPSILON)
        k_inv = lax.rsqrt(jnp.mean(k * k, axis=1, keepdims=True) + EPSILON)
        q_unit = q * q_inv
        k_unit = k * k_inv
        q_norm = (q_unit * q_gain).astype(jnp.bfloat16)
        k_norm = (k_unit * k_gain).astype(jnp.bfloat16)
        rowrow = (((1,), (1,)), ((), ()))
        colcol = (((0,), (0,)), ((), ()))
        dot = functools.partial(lax.dot_general, preferred_element_type=jnp.float32)
        scores = dot(q_norm, k_norm, rowrow) * factor + bias[...]
        highest = jnp.max(scores, axis=1, keepdims=True)
        powers = jnp.exp(scores - highest)
        summed = jnp.sum(powers, axis=1, keepdims=True)
        weights = powers * (owned[...] / summed)
        half_weights = weights.astype(jnp.bfloat16)
        attended = jnp.dot(half_weights, v, preferred_element_type=jnp.float32)
        attended = attended.astype(jnp.bfloat16).astype(jnp.float32)
        row_dot = jnp.sum(grad.astype(jnp.float32) * attended, axis=1, keepdims=True)
        grad_weights = dot(grad, v, rowrow)
        grad_scores = (weights * (grad_weights - row_dot)).astype(jnp.bfloat16)
        dq = jnp.dot(grad_scores, k_norm, preferred_element_type=jnp.float32) * factor
        dk = dot(grad_scores, q_norm, colcol) * factor
        dv = dot(half_weights, grad, colcol).astype(jnp.bfloat16)
        gain_acc[0:1] += jnp.sum(dq * q_unit, axis=0, keepdims=True)
        gain_acc[1:2] += jnp.sum(dk * k_unit, axis=0, keepdims=True)
        dq = norm_back(dq, q_unit, q_inv, q_gain)
        dk = norm_back(dk, k_unit, k_inv, k_gain)
        for a, out in enumerate((dq, dk, dv)):
            ret_send[0, a, :, cols] = out[:half]
            own_out[a, :, cols] = out[half:half + rows]
            ret_send[1, a, :, cols] = out[half + rows:]

    @pl.loop(0, steps)
    def _(step):
        @pl.when(has_left)
        def _():
            for a in range(4):
                to_right(a, step).wait_recv()

        @pl.when(has_right)
        def _():
            for a in range(4):
                to_left(a, step).wait_recv()

        for i in range(HEADS_STEP):
            one_head(step * HEADS_STEP + i)

        @pl.when(has_right)
        def _():
            back_right(step).start()

        @pl.when(has_left)
        def _():
            back_left(step).start()

    seq_gain[me] = gain_acc[...]
    for d in range(1, n_seq):
        peer = lax.rem(me + d, n_seq)
        pltpu.make_async_remote_copy(
            seq_gain.at[me], seq_gain.at[me], seq_send_sem.at[d], seq_recv_sem.at[me],
            device_id={"seq": peer},
        ).start()

    def stores(step):
        return [
            pltpu.make_async_copy(
                own_out.at[a, :, columns(step)],
                outputs[a].at[0, :, columns(step)],
                store_sem.at[step, a],
            )
            for a in range(3)
        ]

    def merge(step):
        @pl.when(has_left)
        def _():
            back_right(step).wait_recv()

        @pl.when(has_right)
        def _():
            back_left(step).wait_recv()

        cols = columns(step)
        own_out[:, 0:half, cols] += ret_recv[0, :, :, cols]
        own_out[:, half:rows, cols] += ret_recv[1, :, :, cols]
        for store in stores(step):
            store.start()

    @pl.loop(0, steps - 1)
    def _(step):
        merge(step)

    summed = jnp.zeros_like(gain_acc)
    for d in range(1, n_seq):
        peer = lax.rem(me + d, n_seq)
        pltpu.make_async_remote_copy(
            seq_gain.at[me], seq_gain.at[peer], seq_send_sem.at[d], seq_recv_sem.at[peer],
            device_id={"seq": peer},
        ).wait()
    for i in range(n_seq):
        summed = summed + seq_gain[i]
    dp_gain[my_dp] = summed
    for d in range(1, n_dp):
        peer = lax.rem(my_dp + d, n_dp)
        pltpu.make_async_remote_copy(
            dp_gain.at[my_dp], dp_gain.at[my_dp], dp_send_sem.at[d], dp_recv_sem.at[my_dp],
            device_id={"dp": peer},
        ).start()

    merge(steps - 1)

    for d in range(1, n_dp):
        peer = lax.rem(my_dp + d, n_dp)
        pltpu.make_async_remote_copy(
            dp_gain.at[my_dp], dp_gain.at[peer], dp_send_sem.at[d], dp_recv_sem.at[peer],
            device_id={"dp": peer},
        ).wait()
    summed = jnp.zeros_like(gain_acc)
    for i in range(n_dp):
        summed = summed + dp_gain[i]
    gain_ref[...] = summed[0:2]

    @pl.loop(0, steps)
    def _(step):
        @pl.when(has_right)
        def _():
            for a in range(4):
                to_right(a, step).wait_send()
            back_right(step).wait_send()

        @pl.when(has_left)
        def _():
            for a in range(4):
                to_left(a, step).wait_send()
            back_left(step).wait_send()

        for store in stores(step):
            store.wait()


def body(query_rows, key_rows, value_rows, out_grad, query_gain, key_gain, lengths):
    rows, width = query_rows.shape[1:]
    half, window = rows // 2, 2 * rows
    samples = lengths.shape[1]
    n_seq, n_dp = lax.axis_size("seq"), lax.axis_size("dp")
    steps = width // (HEADS_STEP * DH)
    big = jax.ShapeDtypeStruct((1, rows, width), jnp.bfloat16)
    anywhere = pl.BlockSpec(memory_space=pl.ANY)
    vmem = pl.BlockSpec(memory_space=pltpu.VMEM)
    dma = pltpu.SemaphoreType.DMA
    return pl.pallas_call(
        functools.partial(kernel, rows, width, samples, n_seq, n_dp),
        out_shape=(big, big, big, jax.ShapeDtypeStruct((2, DH), jnp.float32)),
        in_specs=[anywhere] * 4 + [vmem] * 2 + [pl.BlockSpec(memory_space=pltpu.SMEM)],
        out_specs=(anywhere, anywhere, anywhere, vmem),
        scratch_shapes=[
            pltpu.VMEM((4, window, width), jnp.bfloat16),
            pltpu.VMEM((window, window), jnp.float32),
            pltpu.VMEM((window, 1), jnp.float32),
            pltpu.VMEM((3, rows, width), jnp.bfloat16),
            pltpu.VMEM((2, 3, half, width), jnp.bfloat16),
            pltpu.VMEM((2, 3, half, width), jnp.bfloat16),
            pltpu.VMEM((8, DH), jnp.float32),
            pltpu.VMEM((n_seq, 8, DH), jnp.float32),
            pltpu.VMEM((n_dp, 8, DH), jnp.float32),
            dma((4,)),
            dma((steps, 4, 2)),
            dma((steps, 4, 2)),
            dma((steps, 2)),
            dma((steps, 2)),
            dma((steps, 3)),
            dma((n_seq,)),
            dma((n_seq,)),
            dma((n_dp,)),
            dma((n_dp,)),
        ],
        compiler_params=pltpu.CompilerParams(collective_id=0, has_side_effects=True),
    )(
        query_rows, key_rows, value_rows, out_grad,
        query_gain.reshape(1, DH), key_gain.reshape(1, DH), lengths,
    )


def solution(mesh):
    placed = (
        P("dp", "seq", None),
        P("dp", "seq", None),
        P("dp", "seq", None),
        P("dp", "seq", None),
        P(),
        P(),
        P("dp", None),
    )
    return jax.shard_map(
        body,
        mesh=mesh,
        in_specs=placed,
        out_specs=(P("dp", "seq", None), P("dp", "seq", None), P("dp", "seq", None), P()),
        check_vma=False,
    )
```

```python
import functools

import jax
import jax.numpy as jnp
from jax import lax
from jax.experimental import pallas as pl
from jax.experimental.pallas import tpu as pltpu
from jax.sharding import PartitionSpec as P

DH = 128
EPSILON = 1e-06
MASKED = -1e30
HEADS_STEP = 2


def norm_back(grad, unit, inverse, gain):
    scaled = grad * gain
    inner = jnp.mean(scaled * unit, axis=1, keepdims=True)
    return (inverse * (scaled - unit * inner)).astype(jnp.bfloat16)


def kernel(
    rows, width, samples, n_seq, n_dp,
    q_ref, k_ref, v_ref, g_ref, qgain_in, kgain_in, len_in,
    dq_ref, dk_ref, dv_ref, gain_ref,
    qgain_ref, kgain_ref, len_ref, win, bias, owned, ret_send, ret_recv, gain_acc, seq_gain, dp_gain,
    load_sem, send_sem, recv_sem, back_send_sem, back_recv_sem,
    seq_send_sem, seq_recv_sem, dp_send_sem, dp_recv_sem,
):
    half = rows // 2
    window = 2 * rows
    cols_step = HEADS_STEP * DH
    steps = width // cols_step
    factor = DH ** (-0.5)
    me = lax.axis_index("seq")
    my_dp = lax.axis_index("dp")
    has_left = me > 0
    has_right = me < n_seq - 1
    inputs = (q_ref, k_ref, v_ref, g_ref)
    outputs = (dq_ref, dk_ref, dv_ref)

    barrier = pltpu.get_barrier_semaphore()
    for d in range(1, n_seq):
        pl.semaphore_signal(barrier, inc=1, device_id={"seq": lax.rem(me + d, n_seq)})
    for d in range(1, n_dp):
        pl.semaphore_signal(barrier, inc=1, device_id={"dp": lax.rem(my_dp + d, n_dp)})

    loads = [
        pltpu.make_async_copy(ref.at[0], win.at[a, pl.ds(half, rows)], load_sem.at[a])
        for a, ref in enumerate(inputs)
    ]
    small = [
        pltpu.make_async_copy(src, dst, load_sem.at[4 + i])
        for i, (src, dst) in enumerate(
            ((len_in, len_ref), (qgain_in, qgain_ref), (kgain_in, kgain_ref))
        )
    ]
    for load in small:
        load.start()
    for load in loads:
        load.start()
    pl.semaphore_wait(barrier, n_seq + n_dp - 2)

    def columns(step):
        return pl.ds(pl.multiple_of(step * cols_step, cols_step), cols_step)

    def to_left(a, step):
        return pltpu.make_async_remote_copy(
            inputs[a].at[0, pl.ds(0, half), columns(step)],
            win.at[a, pl.ds(half + rows, half), columns(step)],
            send_sem.at[step, a, 0], recv_sem.at[step, a, 1],
            device_id={"seq": me - 1},
        )

    def to_right(a, step):
        return pltpu.make_async_remote_copy(
            inputs[a].at[0, pl.ds(half, half), columns(step)],
            win.at[a, pl.ds(0, half), columns(step)],
            send_sem.at[step, a, 1], recv_sem.at[step, a, 0],
            device_id={"seq": me + 1},
        )

    def back_left(step):
        return pltpu.make_async_remote_copy(
            ret_send.at[0, :, :, columns(step)],
            ret_recv.at[1, :, :, columns(step)],
            back_send_sem.at[step, 0], back_recv_sem.at[step, 1],
            device_id={"seq": me - 1},
        )

    def back_right(step):
        return pltpu.make_async_remote_copy(
            ret_send.at[1, :, :, columns(step)],
            ret_recv.at[0, :, :, columns(step)],
            back_send_sem.at[step, 1], back_recv_sem.at[step, 0],
            device_id={"seq": me + 1},
        )

    @pl.loop(0, steps)
    def _(step):
        @pl.when(has_right)
        def _():
            for a in range(4):
                to_right(a, step).start()

        @pl.when(has_left)
        def _():
            for a in range(4):
                to_left(a, step).start()

    @pl.when(jnp.logical_not(has_left))
    def _():
        win[:, 0:half, :] = jnp.zeros((4, half, width), jnp.bfloat16)
        ret_recv[0] = jnp.zeros((3, half, width), jnp.bfloat16)

    @pl.when(jnp.logical_not(has_right))
    def _():
        win[:, half + rows:, :] = jnp.zeros((4, half, width), jnp.bfloat16)
        ret_recv[1] = jnp.zeros((3, half, width), jnp.bfloat16)

    for load in small:
        load.wait()
    first = me * rows
    base = first - half
    far = rows * n_seq + window
    pos_col = base + lax.broadcasted_iota(jnp.int32, (window, 1), 0)
    pos_row = base + lax.broadcasted_iota(jnp.int32, (1, window), 1)
    start_col = jnp.where(pos_col >= 0, 0, -far)
    start_row = jnp.where(pos_row >= 0, 0, -far)
    end_col = jnp.full((window, 1), far, jnp.int32)
    total = jnp.int32(0)
    for s in range(samples):
        total = total + len_ref[0, s]
        start_col = jnp.where(total <= pos_col, total, start_col)
        start_row = jnp.where(total <= pos_row, total, start_row)
        end_col = jnp.where(total > pos_col, jnp.minimum(end_col, total), end_col)
    anchor = jnp.minimum(start_col + half, end_col - 1)
    mine = (anchor >= first) & (anchor < first + rows)
    owned[...] = jnp.where(mine, 1.0, 0.0)
    bias[...] = jnp.where(start_col == start_row, 0.0, MASKED)
    gain_acc[...] = jnp.zeros_like(gain_acc)

    for load in loads:
        load.wait()

    def one_head(head):
        cols = pl.ds(pl.multiple_of(head * DH, DH), DH)
        q_gain = qgain_ref[...]
        k_gain = kgain_ref[...]
        q = win[0, :, cols].astype(jnp.float32)
        k = win[1, :, cols].astype(jnp.float32)
        v = win[2, :, cols]
        grad = win[3, :, cols]
        q_inv = lax.rsqrt(jnp.mean(q * q, axis=1, keepdims=True) + EPSILON)
        k_inv = lax.rsqrt(jnp.mean(k * k, axis=1, keepdims=True) + EPSILON)
        q_unit = q * q_inv
        k_unit = k * k_inv
        q_norm = (q_unit * q_gain).astype(jnp.bfloat16)
        k_norm = (k_unit * k_gain).astype(jnp.bfloat16)
        rowrow = (((1,), (1,)), ((), ()))
        colcol = (((0,), (0,)), ((), ()))
        dot = functools.partial(lax.dot_general, preferred_element_type=jnp.float32)
        scores = dot(q_norm, k_norm, rowrow) * factor + bias[...]
        highest = jnp.max(scores, axis=1, keepdims=True)
        powers = jnp.exp(scores - highest)
        summed = jnp.sum(powers, axis=1, keepdims=True)
        weights = powers * (owned[...] / summed)
        half_weights = weights.astype(jnp.bfloat16)
        attended = jnp.dot(half_weights, v, preferred_element_type=jnp.float32)
        attended = attended.astype(jnp.bfloat16).astype(jnp.float32)
        row_dot = jnp.sum(grad.astype(jnp.float32) * attended, axis=1, keepdims=True)
        grad_weights = dot(grad, v, rowrow)
        grad_scores = (weights * (grad_weights - row_dot)).astype(jnp.bfloat16)
        dq = jnp.dot(grad_scores, k_norm, preferred_element_type=jnp.float32) * factor
        dk = dot(grad_scores, q_norm, colcol) * factor
        dv = dot(half_weights, grad, colcol).astype(jnp.bfloat16)
        gain_acc[0:1] += jnp.sum(dq * q_unit, axis=0, keepdims=True)
        gain_acc[1:2] += jnp.sum(dk * k_unit, axis=0, keepdims=True)
        dq = norm_back(dq, q_unit, q_inv, q_gain)
        dk = norm_back(dk, k_unit, k_inv, k_gain)
        for a, out in enumerate((dq, dk, dv)):
            ret_send[0, a, :, cols] = out[:half]
            outputs[a][0, :, cols] = out[half:half + rows]
            ret_send[1, a, :, cols] = out[half + rows:]

    @pl.loop(0, steps)
    def _(step):
        @pl.when(has_left)
        def _():
            for a in range(4):
                to_right(a, step).wait_recv()

        @pl.when(has_right)
        def _():
            for a in range(4):
                to_left(a, step).wait_recv()

        for i in range(HEADS_STEP):
            one_head(step * HEADS_STEP + i)

        @pl.when(has_right)
        def _():
            back_right(step).start()

        @pl.when(has_left)
        def _():
            back_left(step).start()

    def exchange(slots, axis, mine, count, send_sems, recv_sems):
        def copy(d, slot):
            return pltpu.make_async_remote_copy(
                slots.at[mine], slots.at[slot], send_sems.at[d], recv_sems.at[slot],
                device_id={axis: lax.rem(mine + d, count)},
            )

        def start():
            for d in range(1, count):
                copy(d, mine).start()

        def wait():
            for d in range(1, count):
                copy(d, lax.rem(mine + d, count)).wait()
            total = slots[0]
            for i in range(1, count):
                total = total + slots[i]
            return total

        return start, wait

    dp_start, dp_wait = exchange(dp_gain, "dp", my_dp, n_dp, dp_send_sem, dp_recv_sem)
    seq_start, seq_wait = exchange(seq_gain, "seq", me, n_seq, seq_send_sem, seq_recv_sem)

    def merge(step):
        @pl.when(has_left)
        def _():
            back_right(step).wait_recv()

        @pl.when(has_right)
        def _():
            back_left(step).wait_recv()

        cols = columns(step)
        for a, out in enumerate(outputs):
            out[0, 0:half, cols] += ret_recv[0, a, :, cols]
            out[0, half:rows, cols] += ret_recv[1, a, :, cols]

    dp_gain[my_dp] = gain_acc[...]
    dp_start()

    @pl.loop(0, steps - 2)
    def _(step):
        merge(step)

    seq_gain[me] = dp_wait()
    seq_start()

    @pl.loop(steps - 2, steps)
    def _(step):
        merge(step)

    gain_ref[...] = seq_wait()

    @pl.loop(0, steps)
    def _(step):
        @pl.when(has_right)
        def _():
            for a in range(4):
                to_right(a, step).wait_send()
            back_right(step).wait_send()

        @pl.when(has_left)
        def _():
            for a in range(4):
                to_left(a, step).wait_send()
            back_left(step).wait_send()


def write_back(dq_in, dk_in, dv_in, gain_in, dq_ref, dk_ref, dv_ref, gain_ref, sem):
    copies = [
        pltpu.make_async_copy(held, out, sem.at[i])
        for i, (held, out) in enumerate(
            ((dq_in, dq_ref), (dk_in, dk_ref), (dv_in, dv_ref), (gain_in, gain_ref))
        )
    ]
    for copy in copies:
        copy.start()
    for copy in copies:
        copy.wait()


def body(query_rows, key_rows, value_rows, out_grad, query_gain, key_gain, lengths):
    rows, width = query_rows.shape[1:]
    half, window = rows // 2, 2 * rows
    samples = lengths.shape[1]
    n_seq, n_dp = lax.axis_size("seq"), lax.axis_size("dp")
    steps = width // (HEADS_STEP * DH)
    big = jax.ShapeDtypeStruct((1, rows, width), jnp.bfloat16)
    anywhere = pl.BlockSpec(memory_space=pl.ANY)
    hbm = pl.BlockSpec(memory_space=pltpu.HBM)
    vmem = pl.BlockSpec(memory_space=pltpu.VMEM)
    dma = pltpu.SemaphoreType.DMA
    limit = 67043328 - 3 * big.size * 2 - 131072
    shapes = (big, big, big, jax.ShapeDtypeStruct((2, DH), jnp.float32))
    results = pl.pallas_call(
        functools.partial(kernel, rows, width, samples, n_seq, n_dp),
        out_shape=tuple(pltpu.VMEM(x.shape, x.dtype) for x in shapes),
        in_specs=[hbm] * 4 + [hbm] * 3,
        out_specs=(vmem, vmem, vmem, vmem),
        scratch_shapes=[
            pltpu.VMEM((1, DH), jnp.float32),
            pltpu.VMEM((1, DH), jnp.float32),
            pltpu.SMEM((1, samples), jnp.int32),
            pltpu.VMEM((4, window, width), jnp.bfloat16),
            pltpu.VMEM((window, window), jnp.float32),
            pltpu.VMEM((window, 1), jnp.float32),
            pltpu.VMEM((2, 3, half, width), jnp.bfloat16),
            pltpu.VMEM((2, 3, half, width), jnp.bfloat16),
            pltpu.VMEM((2, DH), jnp.float32),
            pltpu.VMEM((n_seq, 2, DH), jnp.float32),
            pltpu.VMEM((n_dp, 2, DH), jnp.float32),
            dma((7,)),
            dma((steps, 4, 2)),
            dma((steps, 4, 2)),
            dma((steps, 2)),
            dma((steps, 2)),
            dma((n_seq,)),
            dma((n_seq,)),
            dma((n_dp,)),
            dma((n_dp,)),
        ],
        compiler_params=pltpu.CompilerParams(collective_id=0, has_side_effects=True, vmem_limit_bytes=limit),
    )(
        query_rows, key_rows, value_rows, out_grad,
        query_gain.reshape(1, DH), key_gain.reshape(1, DH), lengths,
    )
    return pl.pallas_call(
        write_back,
        out_shape=shapes,
        in_specs=[anywhere] * 4,
        out_specs=(anywhere,) * 4,
        scratch_shapes=[dma((4,))],
        compiler_params=pltpu.CompilerParams(vmem_limit_bytes=8 << 20),
    )(*results)


def solution(mesh):
    placed = (
        P("dp", "seq", None),
        P("dp", "seq", None),
        P("dp", "seq", None),
        P("dp", "seq", None),
        P(),
        P(),
        P("dp", None),
    )
    return jax.shard_map(
        body,
        mesh=mesh,
        in_specs=placed,
        out_specs=(P("dp", "seq", None), P("dp", "seq", None), P("dp", "seq", None), P()),
        check_vma=False,
    )
```

```python
import functools

import jax
import jax.numpy as jnp
from jax import lax
from jax.experimental import pallas as pl
from jax.experimental.pallas import tpu as pltpu
from jax.sharding import PartitionSpec as P

DH = 128
EPSILON = 1e-06
MASKED = -1e30
HEADS_STEP = 3


def norm_back(grad, unit, inverse, gain):
    scaled = grad * gain
    inner = jnp.mean(scaled * unit, axis=1, keepdims=True)
    return (inverse * (scaled - unit * inner)).astype(jnp.bfloat16)


def kernel(
    rows, width, samples, n_seq, n_dp,
    q_ref, k_ref, v_ref, g_ref, qgain_in, kgain_in, len_in,
    dq_ref, dk_ref, dv_ref, gain_ref,
    qgain_ref, kgain_ref, len_ref, win, bias, owned, ret_send, ret_recv, gain_acc, seq_gain, dp_gain,
    load_sem, send_sem, recv_sem, back_send_sem, back_recv_sem,
    seq_send_sem, seq_recv_sem, dp_send_sem, dp_recv_sem,
):
    half = rows // 2
    window = 2 * rows
    cols_step = HEADS_STEP * DH
    steps = width // cols_step
    factor = DH ** (-0.5)
    me = lax.axis_index("seq")
    my_dp = lax.axis_index("dp")
    has_left = me > 0
    has_right = me < n_seq - 1
    inputs = (q_ref, k_ref, v_ref, g_ref)
    outputs = (dq_ref, dk_ref, dv_ref)

    barrier = pltpu.get_barrier_semaphore()
    for d in range(1, n_seq):
        pl.semaphore_signal(barrier, inc=1, device_id={"seq": lax.rem(me + d, n_seq)})
    for d in range(1, n_dp):
        pl.semaphore_signal(barrier, inc=1, device_id={"dp": lax.rem(my_dp + d, n_dp)})

    loads = [
        pltpu.make_async_copy(ref.at[0], win.at[a, pl.ds(half, rows)], load_sem.at[a])
        for a, ref in enumerate(inputs)
    ]
    small = [
        pltpu.make_async_copy(src, dst, load_sem.at[4 + i])
        for i, (src, dst) in enumerate(
            ((len_in, len_ref), (qgain_in, qgain_ref), (kgain_in, kgain_ref))
        )
    ]
    for load in small:
        load.start()
    for load in loads:
        load.start()
    pl.semaphore_wait(barrier, n_seq + n_dp - 2)

    def columns(step):
        return pl.ds(pl.multiple_of(step * cols_step, cols_step), cols_step)

    def to_left(a, step):
        return pltpu.make_async_remote_copy(
            inputs[a].at[0, pl.ds(0, half), columns(step)],
            win.at[a, pl.ds(half + rows, half), columns(step)],
            send_sem.at[step, a, 0], recv_sem.at[step, a, 1],
            device_id={"seq": me - 1},
        )

    def to_right(a, step):
        return pltpu.make_async_remote_copy(
            inputs[a].at[0, pl.ds(half, half), columns(step)],
            win.at[a, pl.ds(0, half), columns(step)],
            send_sem.at[step, a, 1], recv_sem.at[step, a, 0],
            device_id={"seq": me + 1},
        )

    def back_left(step):
        return pltpu.make_async_remote_copy(
            ret_send.at[0, :, :, columns(step)],
            ret_recv.at[1, :, :, columns(step)],
            back_send_sem.at[step, 0], back_recv_sem.at[step, 1],
            device_id={"seq": me - 1},
        )

    def back_right(step):
        return pltpu.make_async_remote_copy(
            ret_send.at[1, :, :, columns(step)],
            ret_recv.at[0, :, :, columns(step)],
            back_send_sem.at[step, 1], back_recv_sem.at[step, 0],
            device_id={"seq": me + 1},
        )

    @pl.loop(0, steps)
    def _(step):
        @pl.when(has_right)
        def _():
            for a in range(4):
                to_right(a, step).start()

        @pl.when(has_left)
        def _():
            for a in range(4):
                to_left(a, step).start()

    @pl.when(jnp.logical_not(has_left))
    def _():
        win[:, 0:half, :] = jnp.zeros((4, half, width), jnp.bfloat16)
        ret_recv[0] = jnp.zeros((3, half, width), jnp.bfloat16)

    @pl.when(jnp.logical_not(has_right))
    def _():
        win[:, half + rows:, :] = jnp.zeros((4, half, width), jnp.bfloat16)
        ret_recv[1] = jnp.zeros((3, half, width), jnp.bfloat16)

    for load in small:
        load.wait()
    first = me * rows
    base = first - half
    far = rows * n_seq + window
    pos_col = base + lax.broadcasted_iota(jnp.int32, (window, 1), 0)
    pos_row = base + lax.broadcasted_iota(jnp.int32, (1, window), 1)
    start_col = jnp.where(pos_col >= 0, 0, -far)
    start_row = jnp.where(pos_row >= 0, 0, -far)
    end_col = jnp.full((window, 1), far, jnp.int32)
    total = jnp.int32(0)
    for s in range(samples):
        total = total + len_ref[0, s]
        start_col = jnp.where(total <= pos_col, total, start_col)
        start_row = jnp.where(total <= pos_row, total, start_row)
        end_col = jnp.where(total > pos_col, jnp.minimum(end_col, total), end_col)
    anchor = jnp.minimum(start_col + half, end_col - 1)
    mine = (anchor >= first) & (anchor < first + rows)
    owned[...] = jnp.where(mine, 1.0, 0.0)
    bias[...] = jnp.where(start_col == start_row, 0.0, MASKED)
    gain_acc[...] = jnp.zeros_like(gain_acc)

    for load in loads:
        load.wait()

    def one_head(head):
        cols = pl.ds(pl.multiple_of(head * DH, DH), DH)
        q_gain = qgain_ref[...]
        k_gain = kgain_ref[...]
        q = win[0, :, cols].astype(jnp.float32)
        k = win[1, :, cols].astype(jnp.float32)
        v = win[2, :, cols]
        grad = win[3, :, cols]
        q_inv = lax.rsqrt(jnp.mean(q * q, axis=1, keepdims=True) + EPSILON)
        k_inv = lax.rsqrt(jnp.mean(k * k, axis=1, keepdims=True) + EPSILON)
        q_unit = q * q_inv
        k_unit = k * k_inv
        q_norm = (q_unit * q_gain).astype(jnp.bfloat16)
        k_norm = (k_unit * k_gain).astype(jnp.bfloat16)
        rowrow = (((1,), (1,)), ((), ()))
        colcol = (((0,), (0,)), ((), ()))
        dot = functools.partial(lax.dot_general, preferred_element_type=jnp.float32)
        scores = dot(q_norm, k_norm, rowrow) * factor + bias[...]
        highest = jnp.max(scores, axis=1, keepdims=True)
        powers = jnp.exp(scores - highest)
        summed = jnp.sum(powers, axis=1, keepdims=True)
        weights = powers * (owned[...] / summed)
        half_weights = weights.astype(jnp.bfloat16)
        attended = jnp.dot(half_weights, v, preferred_element_type=jnp.float32)
        attended = attended.astype(jnp.bfloat16).astype(jnp.float32)
        row_dot = jnp.sum(grad.astype(jnp.float32) * attended, axis=1, keepdims=True)
        grad_weights = dot(grad, v, rowrow)
        grad_scores = (weights * (grad_weights - row_dot)).astype(jnp.bfloat16)
        dq = jnp.dot(grad_scores, k_norm, preferred_element_type=jnp.float32)
        dk = dot(grad_scores, q_norm, colcol)
        dv = dot(half_weights, grad, colcol).astype(jnp.bfloat16)
        gain_acc[0:1] += jnp.sum(dq * q_unit, axis=0, keepdims=True)
        gain_acc[1:2] += jnp.sum(dk * k_unit, axis=0, keepdims=True)
        dq = norm_back(dq, q_unit, q_inv, q_gain * factor)
        dk = norm_back(dk, k_unit, k_inv, k_gain * factor)
        for a, out in enumerate((dq, dk, dv)):
            ret_send[0, a, :, cols] = out[:half]
            outputs[a][0, :, cols] = out[half:half + rows]
            ret_send[1, a, :, cols] = out[half + rows:]

    @pl.loop(0, steps)
    def _(step):
        @pl.when(has_left)
        def _():
            for a in range(4):
                to_right(a, step).wait_recv()

        @pl.when(has_right)
        def _():
            for a in range(4):
                to_left(a, step).wait_recv()

        for i in range(HEADS_STEP):
            one_head(step * HEADS_STEP + i)

        @pl.when(has_right)
        def _():
            back_right(step).start()

        @pl.when(has_left)
        def _():
            back_left(step).start()

    def exchange(slots, axis, mine, count, send_sems, recv_sems):
        def copy(d, slot):
            return pltpu.make_async_remote_copy(
                slots.at[mine], slots.at[slot], send_sems.at[d], recv_sems.at[slot],
                device_id={axis: lax.rem(mine + d, count)},
            )

        def start():
            for d in range(1, count):
                copy(d, mine).start()

        def wait():
            for d in range(1, count):
                copy(d, lax.rem(mine + d, count)).wait()
            total = slots[0]
            for i in range(1, count):
                total = total + slots[i]
            return total

        return start, wait

    dp_start, dp_wait = exchange(dp_gain, "dp", my_dp, n_dp, dp_send_sem, dp_recv_sem)
    seq_start, seq_wait = exchange(seq_gain, "seq", me, n_seq, seq_send_sem, seq_recv_sem)

    def merge(step):
        @pl.when(has_left)
        def _():
            back_right(step).wait_recv()

        @pl.when(has_right)
        def _():
            back_left(step).wait_recv()

        cols = columns(step)
        for a, out in enumerate(outputs):
            out[0, 0:half, cols] += ret_recv[0, a, :, cols]
            out[0, half:rows, cols] += ret_recv[1, a, :, cols]

    dp_gain[my_dp] = gain_acc[...] * factor
    dp_start()

    @pl.loop(0, steps - 2)
    def _(step):
        merge(step)

    seq_gain[me] = dp_wait()
    seq_start()

    @pl.loop(steps - 2, steps)
    def _(step):
        merge(step)

    gain_ref[...] = seq_wait()

    @pl.loop(0, steps)
    def _(step):
        @pl.when(has_right)
        def _():
            for a in range(4):
                to_right(a, step).wait_send()
            back_right(step).wait_send()

        @pl.when(has_left)
        def _():
            for a in range(4):
                to_left(a, step).wait_send()
            back_left(step).wait_send()


def write_back(dq_in, dk_in, dv_in, gain_in, dq_ref, dk_ref, dv_ref, gain_ref, sem):
    copies = [
        pltpu.make_async_copy(held, out, sem.at[i])
        for i, (held, out) in enumerate(
            ((dq_in, dq_ref), (dk_in, dk_ref), (dv_in, dv_ref), (gain_in, gain_ref))
        )
    ]
    for copy in copies:
        copy.start()
    for copy in copies:
        copy.wait()


def body(query_rows, key_rows, value_rows, out_grad, query_gain, key_gain, lengths):
    rows, width = query_rows.shape[1:]
    half, window = rows // 2, 2 * rows
    samples = lengths.shape[1]
    n_seq, n_dp = lax.axis_size("seq"), lax.axis_size("dp")
    steps = width // (HEADS_STEP * DH)
    big = jax.ShapeDtypeStruct((1, rows, width), jnp.bfloat16)
    anywhere = pl.BlockSpec(memory_space=pl.ANY)
    hbm = pl.BlockSpec(memory_space=pltpu.HBM)
    vmem = pl.BlockSpec(memory_space=pltpu.VMEM)
    dma = pltpu.SemaphoreType.DMA
    limit = 67043328 - 3 * big.size * 2 - 131072
    shapes = (big, big, big, jax.ShapeDtypeStruct((2, DH), jnp.float32))
    results = pl.pallas_call(
        functools.partial(kernel, rows, width, samples, n_seq, n_dp),
        out_shape=tuple(pltpu.VMEM(x.shape, x.dtype) for x in shapes),
        in_specs=[hbm] * 4 + [hbm] * 3,
        out_specs=(vmem, vmem, vmem, vmem),
        scratch_shapes=[
            pltpu.VMEM((1, DH), jnp.float32),
            pltpu.VMEM((1, DH), jnp.float32),
            pltpu.SMEM((1, samples), jnp.int32),
            pltpu.VMEM((4, window, width), jnp.bfloat16),
            pltpu.VMEM((window, window), jnp.float32),
            pltpu.VMEM((window, 1), jnp.float32),
            pltpu.VMEM((2, 3, half, width), jnp.bfloat16),
            pltpu.VMEM((2, 3, half, width), jnp.bfloat16),
            pltpu.VMEM((2, DH), jnp.float32),
            pltpu.VMEM((n_seq, 2, DH), jnp.float32),
            pltpu.VMEM((n_dp, 2, DH), jnp.float32),
            dma((7,)),
            dma((steps, 4, 2)),
            dma((steps, 4, 2)),
            dma((steps, 2)),
            dma((steps, 2)),
            dma((n_seq,)),
            dma((n_seq,)),
            dma((n_dp,)),
            dma((n_dp,)),
        ],
        compiler_params=pltpu.CompilerParams(collective_id=0, has_side_effects=True, vmem_limit_bytes=limit),
    )(
        query_rows, key_rows, value_rows, out_grad,
        query_gain.reshape(1, DH), key_gain.reshape(1, DH), lengths,
    )
    return pl.pallas_call(
        write_back,
        out_shape=shapes,
        in_specs=[anywhere] * 4,
        out_specs=(anywhere,) * 4,
        scratch_shapes=[dma((4,))],
        compiler_params=pltpu.CompilerParams(vmem_limit_bytes=8 << 20),
    )(*results)


def solution(mesh):
    placed = (
        P("dp", "seq", None),
        P("dp", "seq", None),
        P("dp", "seq", None),
        P("dp", "seq", None),
        P(),
        P(),
        P("dp", None),
    )
    return jax.shard_map(
        body,
        mesh=mesh,
        in_specs=placed,
        out_specs=(P("dp", "seq", None), P("dp", "seq", None), P("dp", "seq", None), P()),
        check_vma=False,
    )
```
